32 devices in a mesh: groups: 2 (over x), img: 16 (over z, y, core).
Axes of the slice: x: 2, y: 2, z: 4, core: 2. Of those that a mesh axis runs over, the one named last changes fastest.
Arguments:
- caches: bfloat16 [32, 768, 1024], P(('groups', 'img')), parts along dimension 0, may hold values from -170 to 170
- owner_slot: int32 [32], P('groups'), parts along dimension 0, may hold values from 0 to 15, each once
- pairs: int32 [32, 2], P('groups'), parts along dimension 0, may hold values from 0 to 15, as said below
- block_mask: int32 [32, 12, 12], P(('groups', 'img')), parts along dimension 0, may hold values from 0 to 1, as said below
- cotangent: bfloat16 [32, 768, 768], P(('groups', 'img')), parts along dimension 0, may hold values from -6 to 6
- embed_weight: bfloat16 [1024, 768], replicated, may hold values from -0.1875 to 0.1875
- query_weight: bfloat16 [768, 512], replicated, may hold values from -2 to 2
- key_weight: bfloat16 [768, 512], replicated, may hold values from -2 to 2
- value_weight: bfloat16 [768, 512], replicated, may hold values from -0.21875 to 0.21875
- out_weight: bfloat16 [768, 512], replicated, may hold values from -0.25 to 0.25
Outputs:
- attended: bfloat16 [32, 768, 768], P(('groups', 'img')), parts along dimension 0
- gradients: float32 [1536, 2048], P(('groups', 'img')), parts along dimension 0
The draws below stay inside these ranges and needn't reach their ends.
There are 2 independent parts, one for each index of `groups`. The reference program is written for one: setup_inputs(seed, part) draws one part's arguments, and reference() takes and returns one part's arrays. A program takes and returns all parts, laid end to end along the dimension named above; an argument that names none is the same for every part. Nothing has to cross between parts.
Inputs may be any that keep to these rules, and one draw needn't show every extreme that they name: `pairs`: each row names two different images. `block_mask`: block (i, i) is live in every pair.
All inputs are finite; a program needn't handle non-finite values.
Results may differ from the reference program's by a relative error of at most 0.012.
Values may be sent and summed in bfloat16 or wider, within the bound.
No kernel may reach another device: no remote copies, remote signals or barrier semaphores. Data moves between devices by JAX's collectives and lax.ppermute only.
A program may use at most 128 MiB of HBM per device.

```python
import math
import jax
import jax.numpy as jnp
from jax import lax

D = 1024
E = 768
HEADS = 8
L = 768
BLOCK = 64
ATT = 512
IMAGES = 16
PAIRS = 16
NB = 12


def draw_caches(key, part):
    tokens = jax.random.truncated_normal(key, -6.0, 6.0, (IMAGES, L, D), jnp.float32)
    return tokens.astype(jnp.bfloat16)


def projection_pair(key):
    base = jax.random.truncated_normal(jax.random.fold_in(key, 7), -6.0, 6.0, (E, ATT), jnp.float32)
    query_part = base / math.sqrt(E)
    other = jax.random.truncated_normal(jax.random.fold_in(key, 9), -6.0, 6.0, (E, ATT), jnp.float32)
    key_part = other / math.sqrt(E)
    return (query_part, key_part)


def draw_query_weight(key, part):
    return projection_pair(key)[0].astype(jnp.bfloat16)


def draw_key_weight(key, part):
    return projection_pair(key)[1].astype(jnp.bfloat16)


def draw_pairs(key, part):
    first, second, third = jax.random.split(key, 3)
    left = jax.random.randint(first, (PAIRS,), 0, IMAGES)
    right = jax.random.randint(second, (PAIRS,), 0, IMAGES)
    query_image = left * right // IMAGES
    offset = jax.random.randint(third, (PAIRS,), 1, IMAGES)
    key_image = (query_image + offset) % IMAGES
    return jnp.stack([query_image, key_image], axis=1).astype(jnp.int32)


def draw_block_mask(key, part):
    first, second = jax.random.split(key, 2)
    level = jax.random.randint(first, (PAIRS, 1, 1), 1, 4)
    rolled = jax.random.randint(second, (PAIRS, NB, NB), 0, 4)
    diagonal = (jnp.arange(NB)[:, None] == jnp.arange(NB)[None, :])[None, :, :]
    return jnp.where((rolled < level) | diagonal, 1, 0).astype(jnp.int32)


def level_of(rng, dims, pieces, low, top_value):
    loudness, own = 1.0, jax.random.fold_in(rng, 6)
    for dim, blocks in pieces:
        steps = jnp.exp(jax.random.uniform(jax.random.fold_in(own, dim), (blocks,), jnp.float32, low / len(pieces), top_value / len(pieces)))
        loudness = loudness * jnp.repeat(steps, dims[dim] // blocks).reshape([-1 if axis == dim else 1 for axis in range(len(dims))])
    return loudness


def normal_values(stream_key, dims, spread, most, cuts=(), kind=jnp.bfloat16):
    drawn = jax.random.normal(stream_key, dims, jnp.float32) * spread
    if len(cuts) > 0:
        drawn = level_of(stream_key, dims, cuts, -0.22, 0.18) * drawn
    return jnp.clip(drawn, min=-most, max=most).astype(kind)


def setup_inputs(seed: int = 0, part: int = 0) -> dict:
    seeds = jax.random.split(jax.random.key(seed), 11)
    part_keys = jax.random.split(jax.random.fold_in(seeds[10], part), 11)
    caches = draw_caches(jax.random.fold_in(jax.random.fold_in(seeds[10], part), 71), part)
    owner_slot = jax.random.permutation(part_keys[1], IMAGES).astype(jnp.int32)
    pairs = draw_pairs(jax.random.fold_in(jax.random.fold_in(seeds[10], part), 71), part)
    block_mask = draw_block_mask(jax.random.fold_in(jax.random.fold_in(seeds[10], part), 71), part)
    cotangent = normal_values(part_keys[4], (PAIRS, L, E), 1.0, 6.0, ((0, 16),))
    embed_weight = normal_values(seeds[5], (D, E), D ** -0.5, 0.1875)
    query_weight = draw_query_weight(jax.random.fold_in(seeds[10], 71), part)
    key_weight = draw_key_weight(jax.random.fold_in(seeds[10], 71), part)
    value_weight = normal_values(seeds[8], (E, ATT), E ** -0.5, 0.21875)
    out_weight = normal_values(seeds[9], (E, ATT), ATT ** -0.5, 0.25)
    return dict(caches=caches, owner_slot=owner_slot, pairs=pairs, block_mask=block_mask, cotangent=cotangent, embed_weight=embed_weight, query_weight=query_weight, key_weight=key_weight, value_weight=value_weight, out_weight=out_weight)


def layer_normed(tokens):
    values_f = tokens.astype(jnp.float32)
    centred = values_f - lax.optimization_barrier(jnp.mean(values_f, axis=-1, keepdims=True))
    spread_sq = lax.optimization_barrier(jnp.mean(centred * centred, axis=-1, keepdims=True))
    return (centred * lax.rsqrt(spread_sq + 1e-06)).astype(jnp.bfloat16)

def split_heads(matrix, heads):
    length, width = matrix.shape
    return matrix.reshape(length, heads, width // heads).transpose(1, 0, 2)

def merge_heads(stacked):
    heads, length, hsize = stacked.shape
    return stacked.transpose(1, 0, 2).reshape(length, heads * hsize)

def pair_pass(query_tokens, key_tokens, mask_blocks, cotangent, query_weight, key_weight, value_weight, out_weight, heads, block):
    query_normed = layer_normed(query_tokens)
    key_normed = layer_normed(key_tokens)
    queries = jnp.dot(query_normed, query_weight, preferred_element_type=jnp.float32).astype(jnp.bfloat16)
    keys_all = jnp.dot(key_normed, key_weight, preferred_element_type=jnp.float32).astype(jnp.bfloat16)
    values_all = jnp.dot(key_normed, value_weight, preferred_element_type=jnp.float32).astype(jnp.bfloat16)
    grad_context = jnp.dot(cotangent, out_weight, preferred_element_type=jnp.float32).astype(jnp.bfloat16)
    live_mask = jnp.repeat(jnp.repeat(mask_blocks, block, axis=0), block, axis=1) > 0
    scaling = 1.0 / math.sqrt(queries.shape[1] // heads)

    def one_head(operands):
        head_query, head_key, head_value, head_grad = operands
        scores = jnp.dot(head_query, head_key.T, preferred_element_type=jnp.float32) * scaling
        masked = jnp.where(live_mask, scores, -jnp.inf)
        row_max = lax.optimization_barrier(jnp.max(masked, axis=1, keepdims=True))
        weights = jnp.exp(masked - row_max)
        probability = weights / lax.optimization_barrier(jnp.sum(weights, axis=1, keepdims=True))
        probability_low = probability.astype(jnp.bfloat16)
        context = jnp.dot(probability_low, head_value, preferred_element_type=jnp.float32).astype(jnp.bfloat16)
        grad_value = jnp.dot(probability_low.T, head_grad, preferred_element_type=jnp.float32).astype(jnp.bfloat16)
        grad_prob = jnp.dot(head_grad, head_value.T, preferred_element_type=jnp.float32)
        inner_sum = lax.optimization_barrier(jnp.sum(probability * grad_prob, axis=1, keepdims=True))
        grad_score = (probability * (grad_prob - inner_sum) * scaling).astype(jnp.bfloat16)
        grad_query = jnp.dot(grad_score, head_key, preferred_element_type=jnp.float32).astype(jnp.bfloat16)
        grad_key = jnp.dot(grad_score.T, head_query, preferred_element_type=jnp.float32).astype(jnp.bfloat16)
        return (context, grad_value, grad_query, grad_key)
    stacked = lax.map(one_head, (split_heads(queries, heads), split_heads(keys_all, heads), split_heads(values_all, heads), split_heads(grad_context, heads)))
    context, grad_value, grad_query, grad_key = [merge_heads(member) for member in stacked]
    attended = (query_tokens.astype(jnp.float32) + jnp.dot(context, out_weight.T, preferred_element_type=jnp.float32)).astype(jnp.bfloat16)
    return (attended, (query_normed, key_normed, grad_query, grad_key, grad_value, cotangent, context))

def gradient_rows(kept, start, count):
    query_normed, key_normed, grad_query, grad_key, grad_value, cotangent, context = kept

    def rows_of(matrix):
        return lax.dynamic_slice_in_dim(matrix, start, count, 1)
    return jnp.concatenate([jnp.dot(rows_of(query_normed).T, grad_query, preferred_element_type=jnp.float32), jnp.dot(rows_of(key_normed).T, grad_key, preferred_element_type=jnp.float32), jnp.dot(rows_of(key_normed).T, grad_value, preferred_element_type=jnp.float32), jnp.dot(rows_of(cotangent).T, context, preferred_element_type=jnp.float32)], axis=1)

def reference(caches, owner_slot, pairs, block_mask, cotangent, embed_weight, query_weight, key_weight, value_weight, out_weight):
    flat = caches.reshape(IMAGES * L, D)
    embedded = jnp.dot(flat, embed_weight, preferred_element_type=jnp.float32).astype(jnp.bfloat16).reshape(IMAGES, L, E)
    slots = owner_slot[pairs]
    inverse = 1.0 / PAIRS

    def per_pair(total, operands):
        slot_pair, mask_blocks, pair_cotangent = operands
        query_tokens = embedded[slot_pair[0]]
        key_tokens = embedded[slot_pair[1]]
        attended, kept = pair_pass(query_tokens, key_tokens, mask_blocks, pair_cotangent, query_weight, key_weight, value_weight, out_weight, HEADS, BLOCK)
        return (total + gradient_rows(kept, 0, E), attended)
    total, attended = lax.scan(per_pair, jnp.zeros((E, 4 * ATT), jnp.float32), (slots, block_mask, cotangent))
    return (attended, total * inverse)
```

```python
import functools
import math

import jax
import jax.numpy as jnp
from jax import lax
from jax.experimental import pallas as pl
from jax.experimental.pallas import tpu as pltpu
from jax.sharding import PartitionSpec as P

HEADS = 8
BLOCK = 64
CHUNK = 256
DEAD = -1e30
F32 = jnp.float32
BF16 = jnp.bfloat16
VMEM = pl.BlockSpec(memory_space=pltpu.VMEM)
SMEM = pl.BlockSpec(memory_space=pltpu.SMEM)


def dot_nn(a, b):
    return lax.dot_general(a, b, (((1,), (0,)), ((), ())), preferred_element_type=F32)


def dot_nt(a, b):
    return lax.dot_general(a, b, (((1,), (1,)), ((), ())), preferred_element_type=F32)


def norm_columns(tokens):
    values_f = tokens.astype(F32)
    width = values_f.shape[0]
    centred = values_f - jnp.sum(values_f, axis=0, keepdims=True) * (1.0 / width)
    spread_sq = jnp.sum(centred * centred, axis=0, keepdims=True) * (1.0 / width)
    return (centred * lax.rsqrt(spread_sq + 1e-06)).astype(BF16)


def pick_body(owner_ref, pairs_ref, shares_ref, query_ref, key_ref):
    count = shares_ref.shape[0]

    def step(p, carry):
        query_ref[p] = shares_ref[owner_ref[pairs_ref[2 * p]]]
        key_ref[p] = shares_ref[owner_ref[pairs_ref[2 * p + 1]]]
        return carry

    lax.fori_loop(0, count, step, 0)


def pick(owner_slot, pairs, shares):
    out = jax.ShapeDtypeStruct(shares.shape, shares.dtype)
    return pl.pallas_call(
        pick_body,
        out_shape=(out, out),
        in_specs=[SMEM, SMEM, VMEM],
        out_specs=(VMEM, VMEM),
        name="pick_shares",
    )(owner_slot, pairs.reshape(-1), shares)


def key_body(heads, token_ref, kw_ref, vw_ref, aug_ref, normed_ref, kt_ref, k_ref, vt_ref, v_ref):
    length = token_ref.shape[1]
    hsize = kw_ref.shape[0] // heads
    for c in range(length // CHUNK):
        cols = pl.ds(c * CHUNK, CHUNK)
        normed = norm_columns(token_ref[:, cols])
        normed_ref[:, cols] = normed
        kt_ref[:, cols] = dot_nn(kw_ref[...], normed).astype(BF16)
        vt_ref[:, cols] = dot_nn(vw_ref[...], normed).astype(BF16)
    for h in range(heads):
        rows = pl.ds(h * hsize, hsize)
        k_ref[h] = jnp.concatenate([kt_ref[rows, :].T, aug_ref[...]], axis=1)
        v_ref[h] = vt_ref[rows, :].T


def key_side(tokens, kw, vw, aug, heads):
    width, length = tokens.shape
    att = kw.shape[0]
    hsize = att // heads
    flat = jax.ShapeDtypeStruct((att, length), BF16)
    return pl.pallas_call(
        functools.partial(key_body, heads),
        out_shape=(
            jax.ShapeDtypeStruct((width, length), BF16),
            flat,
            jax.ShapeDtypeStruct((heads, length, 2 * hsize), BF16),
            flat,
            jax.ShapeDtypeStruct((heads, length, hsize), BF16),
        ),
        in_specs=[VMEM] * 4,
        out_specs=(VMEM,) * 5,
        compiler_params=pltpu.CompilerParams(vmem_limit_bytes=40 * 2**20),
        name="key_side",
    )(tokens, kw, vw, aug)


def chunk_body(
    heads, first, last, token_ref, qw_ref, hot_ref, gt_ref, g_ref, cot_ref, knt_ref,
    kt_ref, k_ref, vt_ref, v_ref, *rest,
):
    if not first:
        gk_in, gv_in, q_in, o_in = rest[:4]
        rest = rest[4:]
    ctx_ref, gk_ref, gv_ref, gradq_ref, grado_ref = rest[:5]
    rest = rest[5:]
    if last:
        gradk_ref, gradv_ref = rest[:2]
        rest = rest[2:]
    qt_ref, qnat_ref, gq_ref = rest
    att = qw_ref.shape[0]
    hsize = att // heads
    normed = norm_columns(token_ref[...])
    qt_ref[...] = dot_nn(qw_ref[...], normed).astype(BF16)
    for h in range(heads):
        qnat_ref[h] = qt_ref[pl.ds(h * hsize, hsize), :].T
    scale = jnp.asarray(1.0 / math.sqrt(hsize), BF16)

    def one_head(h, carry):
        rows = pl.ds(pl.multiple_of(h * hsize, hsize), hsize)
        query_aug = jnp.concatenate([qt_ref[rows, :] * scale, hot_ref[...]], axis=0)
        scores = dot_nn(k_ref[h], query_aug)
        top = jnp.max(scores, axis=0, keepdims=True)
        weights = jnp.exp(scores - top)
        total = jnp.sum(weights, axis=0, keepdims=True)
        prob = weights * (1.0 / total)
        low = prob.astype(BF16)
        ctx_ref[rows, :] = dot_nn(vt_ref[rows, :], low).astype(BF16)
        grad_prob = dot_nn(v_ref[h], gt_ref[rows, :] * scale)
        inner = jnp.sum(prob * grad_prob, axis=0, keepdims=True)
        grad_score = (prob * (grad_prob - inner)).astype(BF16)
        gq_ref[rows, :] = dot_nn(kt_ref[rows, :], grad_score).astype(BF16)
        gv = dot_nn(low, g_ref[h])
        gk = dot_nn(grad_score, qnat_ref[h])
        if first:
            gv_ref[h] = gv
            gk_ref[h] = gk
        else:
            gv_ref[h] = gv_in[h] + gv
            gk_ref[h] = gk_in[h] + gk
        return carry

    lax.fori_loop(0, heads, one_head, 0)
    gradq = dot_nt(normed, gq_ref[...])
    grado = dot_nt(cot_ref[...], ctx_ref[...])
    gradq_ref[...] = gradq if first else q_in[...] + gradq
    grado_ref[...] = grado if first else o_in[...] + grado
    if last:
        for out_ref, acc_ref in ((gradk_ref, gk_ref), (gradv_ref, gv_ref)):
            merged = jnp.concatenate([acc_ref[h].astype(BF16) for h in range(heads)], axis=1)
            out_ref[...] = dot_nn(knt_ref[...], merged)


def chunk_side(index, count, tokens, qw, hot, gt, g, cot, key_state, carried, heads):
    knt, kt, k, vt, v = key_state
    width, chunk = tokens.shape
    length = knt.shape[1]
    att = qw.shape[0]
    hsize = att // heads
    first, last = index == 0, index == count - 1
    acc = jax.ShapeDtypeStruct((heads, length, hsize), F32)
    grad = jax.ShapeDtypeStruct((width, att), F32)
    outs = [jax.ShapeDtypeStruct((att, chunk), BF16), acc, acc, grad, grad]
    if last:
        outs += [grad, grad]
    args = [tokens, qw, hot, gt, g, cot, knt, kt, k, vt, v]
    alias = {}
    if not first:
        alias = {len(args) + n: n + 1 for n in range(4)}
        args += list(carried)
    return pl.pallas_call(
        functools.partial(chunk_body, heads, first, last),
        out_shape=tuple(outs),
        in_specs=[VMEM] * len(args),
        out_specs=(VMEM,) * len(outs),
        scratch_shapes=[
            pltpu.VMEM((att, chunk), BF16),
            pltpu.VMEM((heads, chunk, hsize), BF16),
            pltpu.VMEM((att, chunk), BF16),
        ],
        input_output_aliases=alias,
        compiler_params=pltpu.CompilerParams(vmem_limit_bytes=56 * 2**20),
        name="attend_chunk",
    )(*args)


def scatter_sum(total, axis):
    size = lax.axis_size(axis)
    me = lax.axis_index(axis)
    rows, cols = total.shape
    part = total.reshape(size, rows // size, cols)
    bit = 1
    while bit < size:
        mine = (me // bit) % 2
        halves = part.reshape(part.shape[0] // 2, 2, *part.shape[1:])
        send = lax.dynamic_index_in_dim(halves, 1 - mine, 1, keepdims=False)
        keep = lax.dynamic_index_in_dim(halves, mine, 1, keepdims=False)
        got = lax.ppermute(send, axis, [(d, d ^ bit) for d in range(size)])
        part = keep + got
        bit *= 2
    return part[0]


def per_device(
    caches, owner_slot, pairs, block_mask, cotangent, embed_weight, query_weight,
    key_weight, value_weight, out_weight,
):
    devices_img = lax.axis_size("img")
    length = caches.shape[1]
    width = embed_weight.shape[1]
    att = query_weight.shape[1]
    hsize = att // HEADS
    blocks = block_mask.shape[1]
    cot = cotangent[0]

    embedded = lax.dot_general(
        embed_weight, caches[0], (((0,), (1,)), ((), ())), preferred_element_type=F32
    ).astype(BF16)
    shares = lax.all_to_all(
        embedded.reshape(devices_img, width // devices_img, length), "img", 0, 0, tiled=True
    )
    query_pick, key_pick = pick(owner_slot, pairs, shares)
    key_tokens = lax.all_to_all(key_pick, "img", 0, 0, tiled=True).reshape(width, length)
    query_tokens = lax.all_to_all(query_pick, "img", 0, 0, tiled=True).reshape(width, length)

    bias = jnp.where(block_mask[0] > 0, 0.0, DEAD).astype(BF16)
    aug = jnp.pad(jnp.repeat(bias.T, BLOCK, axis=0), ((0, 0), (0, hsize - blocks)))
    hot = (
        lax.broadcasted_iota(jnp.int32, (hsize, length), 0)
        == lax.broadcasted_iota(jnp.int32, (hsize, length), 1) // BLOCK
    ).astype(BF16)
    grad_context = jnp.dot(cot, out_weight, preferred_element_type=F32).astype(BF16)
    gt = grad_context.T
    g = grad_context.reshape(length, HEADS, hsize).transpose(1, 0, 2)
    cot_t = cot.T

    key_state = key_side(key_tokens, key_weight.T, value_weight.T, aug, HEADS)
    count = length // CHUNK
    carried, contexts = None, []
    for n in range(count):
        cols = slice(n * CHUNK, (n + 1) * CHUNK)
        out = chunk_side(
            n, count, query_tokens[:, cols], query_weight.T, hot[:, cols], gt[:, cols],
            g[:, cols], cot_t[:, cols], key_state, carried, HEADS,
        )
        contexts.append(out[0])
        carried = out[1:5]
    grad_q, grad_o = carried[2], carried[3]
    grad_k, grad_v = out[5], out[6]
    context = jnp.concatenate(contexts, axis=1)
    total = jnp.concatenate([grad_q, grad_k, grad_v, grad_o], axis=1)
    summed = scatter_sum(total, "img")
    attended = (
        query_tokens.T.astype(F32)
        + lax.dot_general(context, out_weight, (((0,), (1,)), ((), ())), preferred_element_type=F32)
    ).astype(BF16)
    return (attended[None], summed * (1.0 / devices_img))


def solution(mesh):
    spread = P(("groups", "img"), None, None)
    placed = (spread, P("groups"), P("groups", None), spread, spread) + (P(),) * 5
    return jax.shard_map(
        per_device,
        mesh=mesh,
        in_specs=placed,
        out_specs=(spread, P(("groups", "img"), None)),
        check_vma=False,
    )
```

```python
import functools
import math

import jax
import jax.numpy as jnp
from jax import lax
from jax.experimental import pallas as pl
from jax.experimental.pallas import tpu as pltpu
from jax.sharding import PartitionSpec as P

HEADS = 8
BLOCK = 64
CHUNK = 256
DEAD = -1e30
F32 = jnp.float32
F16 = jnp.float16
BF16 = jnp.bfloat16
VMEM = pl.BlockSpec(memory_space=pltpu.VMEM)
SMEM = pl.BlockSpec(memory_space=pltpu.SMEM)


def dot_nn(a, b):
    return lax.dot_general(a, b, (((1,), (0,)), ((), ())), preferred_element_type=F32)


def dot_nt(a, b):
    return lax.dot_general(a, b, (((1,), (1,)), ((), ())), preferred_element_type=F32)


def norm_columns(tokens):
    values_f = tokens.astype(F32)
    width = values_f.shape[0]
    centred = values_f - jnp.sum(values_f, axis=0, keepdims=True) * (1.0 / width)
    spread_sq = jnp.sum(centred * centred, axis=0, keepdims=True) * (1.0 / width)
    return (centred * lax.rsqrt(spread_sq + 1e-06)).astype(BF16)


def pick_body(owner_ref, pairs_ref, shares_ref, out_ref):
    count = shares_ref.shape[0]

    def step(p, carry):
        for side in range(2):
            out_ref[p, side] = shares_ref[owner_ref[pairs_ref[2 * p + side]]]
        return carry

    lax.fori_loop(0, count, step, 0, unroll=4)


def pick(owner_slot, pairs, shares):
    count = shares.shape[0]
    return pl.pallas_call(
        pick_body,
        out_shape=jax.ShapeDtypeStruct((count, 2) + shares.shape[1:], shares.dtype),
        in_specs=[SMEM, SMEM, VMEM],
        out_specs=VMEM,
        compiler_params=pltpu.CompilerParams(vmem_limit_bytes=16 * 2**20),
        name="pick_shares",
    )(owner_slot, pairs.reshape(-1), shares)


def pair_body(
    heads, core_ref, token_ref, qw_ref, kw_ref, vw_ref, aug_ref, hot_ref, gt_ref, g_ref, cot_ref,
    ctx_ref, keep_qk_ref, send_qk_ref, keep_vo_ref, send_vo_ref,
    qn_ref, kn_ref, qt_ref, kt_ref, vt_ref, q_ref, k_ref, v_ref, gq_ref, gk_ref, gv_ref, val_ref,
):
    count, _, share, length = token_ref.shape
    att = qw_ref.shape[0]
    hsize = att // heads
    scale = jnp.asarray(1.0 / math.sqrt(hsize), BF16)
    for c in range(length // CHUNK):
        cols = pl.ds(c * CHUNK, CHUNK)
        query_n = norm_columns(token_ref[:, 0, :, cols].reshape(count * share, CHUNK))
        key_n = norm_columns(token_ref[:, 1, :, cols].reshape(count * share, CHUNK))
        qn_ref[:, cols] = query_n
        kn_ref[:, cols] = key_n
        qt_ref[:, cols] = dot_nn(qw_ref[...], query_n).astype(BF16)
        kt_ref[:, cols] = dot_nn(kw_ref[...], key_n).astype(BF16)
        vt_ref[:, cols] = dot_nn(vw_ref[...], key_n).astype(BF16)
    for h in range(heads):
        rows = pl.ds(h * hsize, hsize)
        q_ref[h] = qt_ref[rows, :].T
        k_ref[h] = jnp.concatenate([kt_ref[rows, :].T, aug_ref[...]], axis=1)
        v_ref[h] = vt_ref[rows, :].T

    def one_head(h):
        rows = pl.ds(pl.multiple_of(h * hsize, hsize), hsize)
        query_aug = jnp.concatenate([qt_ref[rows, :] * scale, hot_ref[...]], axis=0)
        scores = dot_nn(k_ref[h], query_aug)
        top = jnp.max(scores, axis=0, keepdims=True)
        weights = jnp.exp(scores - top)
        total = jnp.sum(weights, axis=0, keepdims=True)
        prob = weights * (1.0 / total)
        low = prob.astype(BF16)
        ctx_ref[rows, :] = dot_nn(vt_ref[rows, :], low).astype(BF16)
        grad_prob = dot_nn(v_ref[h], gt_ref[rows, :] * scale)
        inner = jnp.sum(prob * grad_prob, axis=0, keepdims=True)
        grad_score = (prob * (grad_prob - inner)).astype(BF16)
        gq_ref[rows, :] = dot_nn(kt_ref[rows, :], grad_score).astype(BF16)
        return (
            dot_nn(grad_score, q_ref[h]).astype(BF16),
            dot_nn(low, g_ref[h]).astype(BF16),
        )

    def two_heads(i, carry):
        gk0, gv0 = one_head(2 * i)
        gk1, gv1 = one_head(2 * i + 1)
        cols = pl.ds(pl.multiple_of(i * 2 * hsize, 2 * hsize), 2 * hsize)
        gk_ref[:, cols] = jnp.concatenate([gk0, gk1], axis=1)
        gv_ref[:, cols] = jnp.concatenate([gv0, gv1], axis=1)
        return carry

    lax.fori_loop(0, heads // 2, two_heads, 0)

    blocks, rows_each, _ = keep_qk_ref.shape
    for n, (left, right, dot) in enumerate(
        (
            (qn_ref, gq_ref, dot_nt),
            (kn_ref, gk_ref, dot_nn),
            (kn_ref, gv_ref, dot_nn),
            (cot_ref, ctx_ref, dot_nt),
        )
    ):
        keep_ref, send_ref = ((keep_qk_ref, send_qk_ref), (keep_vo_ref, send_vo_ref))[n // 2]
        cols = pl.ds((n % 2) * att, att)
        val_ref[...] = dot(left[...], right[...])
        for core, targets in ((0, (keep_ref, send_ref)), (1, (send_ref, keep_ref))):

            @pl.when(core_ref[0] == core)
            def _():
                for b in range(2 * blocks):
                    targets[b % 2][b // 2, :, cols] = val_ref[pl.ds(b * rows_each, rows_each), :]


def pair_side(core, arrived, qw, kw, vw, aug, hot, gt, g, cot, heads, rows_each):
    length = arrived.shape[-1]
    width = cot.shape[0]
    att = qw.shape[0]
    hsize = att // heads
    part = jax.ShapeDtypeStruct((width // rows_each // 2, rows_each, 2 * att), F32)
    flat = pltpu.VMEM((att, length), BF16)
    each = pltpu.VMEM((heads, length, hsize), BF16)
    side = pltpu.VMEM((length, att), BF16)
    return pl.pallas_call(
        functools.partial(pair_body, heads),
        out_shape=(jax.ShapeDtypeStruct((att, length), BF16), part, part, part, part),
        in_specs=[SMEM] + [VMEM] * 9,
        out_specs=(VMEM,) * 5,
        scratch_shapes=[
            pltpu.VMEM((width, length), BF16),
            pltpu.VMEM((width, length), BF16),
            flat,
            flat,
            flat,
            each,
            pltpu.VMEM((heads, length, 2 * hsize), BF16),
            each,
            flat,
            side,
            side,
            pltpu.VMEM((width, att), F32),
        ],
        compiler_params=pltpu.CompilerParams(vmem_limit_bytes=58 * 2**20),
        name="pair_pass",
    )(core, arrived, qw, kw, vw, aug, hot, gt, g, cot)


def exchange(array, axis, bit):
    size = lax.axis_size(axis)
    return lax.ppermute(array, axis, [(d, d ^ (1 << bit)) for d in range(size)])


def scatter_sum(keep, send, axis, order):
    bits = lax.axis_size(axis).bit_length() - 1
    me = lax.axis_index(axis)
    part = keep + exchange(send, axis, 0)
    rows, cols = part.shape[1:]
    part = part.reshape((2,) * (bits - 1) + (rows, cols))
    left = list(reversed(range(1, bits)))
    for bit in order:
        at = left.index(bit)
        left.pop(at)
        mine = (me >> bit) & 1
        send = lax.dynamic_index_in_dim(part, 1 - mine, at, keepdims=False)
        keep = lax.dynamic_index_in_dim(part, mine, at, keepdims=False)
        top = jnp.max(jnp.abs(send), axis=tuple(range(send.ndim - 1)), keepdims=True)
        power = jnp.ceil(jnp.log2(jnp.maximum(top, 1e-30)))
        scaled = (send * jnp.exp2(8.0 - power)).astype(F16)
        power = exchange(power, axis, bit)
        part = keep + exchange(scaled, axis, bit).astype(F32) * jnp.exp2(power - 8.0)
    return part


def per_device(
    caches, owner_slot, pairs, block_mask, cotangent, embed_weight, query_weight,
    key_weight, value_weight, out_weight,
):
    devices_img = lax.axis_size("img")
    bits = devices_img.bit_length() - 1
    length = caches.shape[1]
    width = embed_weight.shape[1]
    att = query_weight.shape[1]
    hsize = att // HEADS
    blocks = block_mask.shape[1]
    cot = cotangent[0]
    share = width // devices_img

    embedded = lax.dot_general(
        embed_weight, caches[0], (((0,), (1,)), ((), ())), preferred_element_type=F32
    ).astype(BF16)
    shares = lax.all_to_all(
        embedded.reshape(devices_img, share, length), "img", 0, 0, tiled=True
    )
    picked = pick(owner_slot, pairs, shares)
    arrived = lax.all_to_all(picked, "img", 0, 0, tiled=True)
    query_tokens = arrived[:, 0].reshape(width, length)
    if share % 16:
        arrived = arrived.transpose(1, 0, 2, 3).reshape(1, 2, width, length)

    bias = jnp.where(block_mask[0] > 0, 0.0, DEAD).astype(BF16)
    aug = jnp.pad(jnp.repeat(bias.T, BLOCK, axis=0), ((0, 0), (0, hsize - blocks)))
    hot = (
        lax.broadcasted_iota(jnp.int32, (hsize, length), 0)
        == lax.broadcasted_iota(jnp.int32, (hsize, length), 1) // BLOCK
    ).astype(BF16)
    grad_context = jnp.dot(cot, out_weight, preferred_element_type=F32).astype(BF16)
    g = grad_context.reshape(length, HEADS, hsize).transpose(1, 0, 2)
    core = (lax.axis_index("img") % 2).astype(jnp.int32).reshape(1)

    context, keep_qk, send_qk, keep_vo, send_vo = pair_side(
        core, arrived, query_weight.T, key_weight.T, value_weight.T, aug, hot,
        grad_context.T, g, cot.T, HEADS, share,
    )
    upward = list(range(1, bits))
    qk = scatter_sum(keep_qk, send_qk, "img", upward)
    vo = scatter_sum(keep_vo, send_vo, "img", upward[1:2] + upward[:1] + upward[2:])
    attended = (
        query_tokens.T.astype(F32)
        + lax.dot_general(context, out_weight, (((0,), (1,)), ((), ())), preferred_element_type=F32)
    ).astype(BF16)
    return (attended[None], jnp.concatenate([qk, vo], axis=1) * (1.0 / devices_img))


def solution(mesh):
    spread = P(("groups", "img"), None, None)
    placed = (spread, P("groups"), P("groups", None), spread, spread) + (P(),) * 5
    return jax.shard_map(
        per_device,
        mesh=mesh,
        in_specs=placed,
        out_specs=(spread, P(("groups", "img"), None)),
        check_vma=False,
    )
```

```python
import functools
import math

import jax
import jax.numpy as jnp
from jax import lax
from jax.experimental import pallas as pl
from jax.experimental.pallas import tpu as pltpu
from jax.sharding import PartitionSpec as P

HEADS = 8
BLOCK = 64
CHUNK = 256
DEAD = -1e30
F32 = jnp.float32
F16 = jnp.float16
BF16 = jnp.bfloat16
VMEM = pl.BlockSpec(memory_space=pltpu.VMEM)
SMEM = pl.BlockSpec(memory_space=pltpu.SMEM)


def dot_nn(a, b):
    return lax.dot_general(a, b, (((1,), (0,)), ((), ())), preferred_element_type=F32)


def dot_nt(a, b):
    return lax.dot_general(a, b, (((1,), (1,)), ((), ())), preferred_element_type=F32)


def norm_columns(tokens):
    values_f = tokens.astype(F32)
    width = values_f.shape[0]
    centred = values_f - jnp.sum(values_f, axis=0, keepdims=True) * (1.0 / width)
    spread_sq = jnp.sum(centred * centred, axis=0, keepdims=True) * (1.0 / width)
    return (centred * lax.rsqrt(spread_sq + 1e-06)).astype(BF16)


def pick_body(owner_ref, pairs_ref, shares_ref, out_ref):
    count = shares_ref.shape[0]

    def step(p, carry):
        for side in range(2):
            out_ref[p, side] = shares_ref[owner_ref[pairs_ref[2 * p + side]]]
        return carry

    lax.fori_loop(0, count, step, 0, unroll=4)


def pick(owner_slot, pairs, shares):
    count = shares.shape[0]
    return pl.pallas_call(
        pick_body,
        out_shape=jax.ShapeDtypeStruct((count, 2) + shares.shape[1:], shares.dtype),
        in_specs=[SMEM, SMEM, VMEM],
        out_specs=VMEM,
        compiler_params=pltpu.CompilerParams(vmem_limit_bytes=16 * 2**20),
        name="pick_shares",
    )(owner_slot, pairs.reshape(-1), shares)


def pair_body(
    heads, core_ref, token_ref, qw_ref, kw_ref, vw_ref, aug_ref, hot_ref, gt_ref, g_ref, cot_ref,
    ctx_ref, keep_ref, send_ref,
    qn_ref, kn_ref, qt_ref, kt_ref, vt_ref, q_ref, k_ref, v_ref, gq_ref, gk_ref, gv_ref, val_ref,
):
    count, _, share, length = token_ref.shape
    att = qw_ref.shape[0]
    hsize = att // heads
    scale = jnp.asarray(1.0 / math.sqrt(hsize), BF16)
    for c in range(length // CHUNK):
        cols = pl.ds(c * CHUNK, CHUNK)
        query_n = norm_columns(token_ref[:, 0, :, cols].reshape(count * share, CHUNK))
        key_n = norm_columns(token_ref[:, 1, :, cols].reshape(count * share, CHUNK))
        qn_ref[:, cols] = query_n
        kn_ref[:, cols] = key_n
        qt_ref[:, cols] = dot_nn(qw_ref[...], query_n).astype(BF16)
        kt_ref[:, cols] = dot_nn(kw_ref[...], key_n).astype(BF16)
        vt_ref[:, cols] = dot_nn(vw_ref[...], key_n).astype(BF16)
    for h in range(heads):
        rows = pl.ds(h * hsize, hsize)
        q_ref[h] = qt_ref[rows, :].T
        k_ref[h] = jnp.concatenate([kt_ref[rows, :].T, aug_ref[...]], axis=1)
        v_ref[h] = vt_ref[rows, :].T

    def rows_of(h):
        return pl.ds(pl.multiple_of(h * hsize, hsize), hsize)

    def scores_of(h):
        query_aug = jnp.concatenate([qt_ref[rows_of(h), :] * scale, hot_ref[...]], axis=0)
        return dot_nn(k_ref[h], query_aug)

    def softmax(scores):
        weights = jnp.exp(scores - jnp.max(scores, axis=0, keepdims=True))
        return weights * (1.0 / jnp.sum(weights, axis=0, keepdims=True))

    def context_of(h, low):
        ctx_ref[rows_of(h), :] = dot_nn(vt_ref[rows_of(h), :], low).astype(BF16)
        return dot_nn(low, g_ref[h]).astype(BF16)

    def grad_score_of(prob, grad_prob):
        inner = jnp.sum(prob * grad_prob, axis=0, keepdims=True)
        return (prob * (grad_prob - inner)).astype(BF16)

    def grads_of(h, grad_score):
        gq_ref[rows_of(h), :] = dot_nn(kt_ref[rows_of(h), :], grad_score).astype(BF16)
        return dot_nn(grad_score, q_ref[h]).astype(BF16)

    def two_heads(i, carry):
        pair = (2 * i, 2 * i + 1)
        cols = pl.ds(pl.multiple_of(i * 2 * hsize, 2 * hsize), 2 * hsize)
        scores = [scores_of(h) for h in pair]
        grad_probs = [dot_nn(v_ref[h], gt_ref[rows_of(h), :] * scale) for h in pair]
        probs = [softmax(each) for each in scores]
        gv_ref[:, cols] = jnp.concatenate(
            [context_of(h, prob.astype(BF16)) for h, prob in zip(pair, probs)], axis=1
        )
        grad_scores = [grad_score_of(*each) for each in zip(probs, grad_probs)]
        gk_ref[:, cols] = jnp.concatenate(
            [grads_of(h, each) for h, each in zip(pair, grad_scores)], axis=1
        )
        return carry

    lax.fori_loop(0, heads // 2, two_heads, 0)

    blocks, rows_each, _ = keep_ref.shape
    for n, (left, right, dot) in enumerate(
        (
            (qn_ref, gq_ref, dot_nt),
            (kn_ref, gk_ref, dot_nn),
            (kn_ref, gv_ref, dot_nn),
            (cot_ref, ctx_ref, dot_nt),
        )
    ):
        cols = pl.ds(n * att, att)
        val_ref[...] = dot(left[...], right[...])
        for core, targets in ((0, (keep_ref, send_ref)), (1, (send_ref, keep_ref))):

            @pl.when(core_ref[0] == core)
            def _():
                for b in range(2 * blocks):
                    targets[b % 2][b // 2, :, cols] = val_ref[pl.ds(b * rows_each, rows_each), :]


def pair_side(core, arrived, qw, kw, vw, aug, hot, gt, g, cot, heads, rows_each):
    length = arrived.shape[-1]
    width = cot.shape[0]
    att = qw.shape[0]
    hsize = att // heads
    part = jax.ShapeDtypeStruct((width // rows_each // 2, rows_each, 4 * att), F32)
    flat = pltpu.VMEM((att, length), BF16)
    each = pltpu.VMEM((heads, length, hsize), BF16)
    side = pltpu.VMEM((length, att), BF16)
    return pl.pallas_call(
        functools.partial(pair_body, heads),
        out_shape=(jax.ShapeDtypeStruct((att, length), BF16), part, part),
        in_specs=[SMEM] + [VMEM] * 9,
        out_specs=(VMEM,) * 3,
        scratch_shapes=[
            pltpu.VMEM((width, length), BF16),
            pltpu.VMEM((width, length), BF16),
            flat,
            flat,
            flat,
            each,
            pltpu.VMEM((heads, length, 2 * hsize), BF16),
            each,
            flat,
            side,
            side,
            pltpu.VMEM((width, att), F32),
        ],
        compiler_params=pltpu.CompilerParams(vmem_limit_bytes=38 * 2**20),
        name="pair_pass",
    )(core, arrived, qw, kw, vw, aug, hot, gt, g, cot)


def exchange(array, axis, bit):
    size = lax.axis_size(axis)
    return lax.ppermute(array, axis, [(d, d ^ (1 << bit)) for d in range(size)])


def out_body(token_ref, ow_ref, ctx_ref, out_ref):
    count, _, share, length = token_ref.shape
    for c in range(length // CHUNK):
        cols = pl.ds(c * CHUNK, CHUNK)
        tokens = token_ref[:, 0, :, cols].reshape(count * share, CHUNK)
        summed = tokens.astype(F32) + dot_nn(ow_ref[...], ctx_ref[:, cols])
        out_ref[cols, :] = summed.astype(BF16).T


def out_side(arrived, ow, context):
    width, att = ow.shape
    length = context.shape[1]
    return pl.pallas_call(
        out_body,
        out_shape=jax.ShapeDtypeStruct((length, width), BF16),
        in_specs=[VMEM] * 3,
        out_specs=VMEM,
        compiler_params=pltpu.CompilerParams(vmem_limit_bytes=24 * 2**20),
        cost_estimate=pl.CostEstimate(
            flops=2 * width * att * length, bytes_accessed=6 * width * length, transcendentals=0
        ),
        name="attended_out",
    )(arrived, ow, context)


def halve(parts, axis, left, bits):
    me = lax.axis_index(axis)
    cut = []
    for part, lefts, bit in zip(parts, left, bits):
        at = lefts.index(bit)
        lefts.pop(at)
        mine = (me >> bit) & 1
        send = lax.dynamic_index_in_dim(part, 1 - mine, at, keepdims=False)
        keep = lax.dynamic_index_in_dim(part, mine, at, keepdims=False)
        top = jnp.max(jnp.abs(send), axis=tuple(range(send.ndim - 1)), keepdims=True)
        power = jnp.ceil(jnp.log2(jnp.maximum(top, 1e-30)))
        cut.append((keep, power, (send * jnp.exp2(8.0 - power)).astype(F16)))
    return cut


def join(cut, axis, bits):
    out = []
    for (keep, power, scaled), bit in zip(cut, bits):
        power = exchange(power, axis, bit)
        out.append(keep + exchange(scaled, axis, bit).astype(F32) * jnp.exp2(power - 8.0))
    return out


def per_device(
    caches, owner_slot, pairs, block_mask, cotangent, embed_weight, query_weight,
    key_weight, value_weight, out_weight,
):
    devices_img = lax.axis_size("img")
    bits = devices_img.bit_length() - 1
    length = caches.shape[1]
    width = embed_weight.shape[1]
    att = query_weight.shape[1]
    hsize = att // HEADS
    blocks = block_mask.shape[1]
    cot = cotangent[0]
    share = width // devices_img

    embedded = lax.dot_general(
        embed_weight, caches[0], (((0,), (1,)), ((), ())), preferred_element_type=F32
    ).astype(BF16)
    shares = lax.all_to_all(
        embedded.reshape(devices_img, share, length), "img", 0, 0, tiled=True
    )
    picked = pick(owner_slot, pairs, shares)
    arrived = lax.all_to_all(picked, "img", 0, 0, tiled=True)
    if share % 16:
        arrived = arrived.transpose(1, 0, 2, 3).reshape(1, 2, width, length)

    bias = jnp.where(block_mask[0] > 0, 0.0, DEAD).astype(BF16)
    aug = jnp.pad(jnp.repeat(bias.T, BLOCK, axis=0), ((0, 0), (0, hsize - blocks)))
    hot = (
        lax.broadcasted_iota(jnp.int32, (hsize, length), 0)
        == lax.broadcasted_iota(jnp.int32, (hsize, length), 1) // BLOCK
    ).astype(BF16)
    grad_context = jnp.dot(cot, out_weight, preferred_element_type=F32).astype(BF16)
    g = grad_context.reshape(length, HEADS, hsize).transpose(1, 0, 2)
    core = (lax.axis_index("img") % 2).astype(jnp.int32).reshape(1)

    context, keep, send = pair_side(
        core, arrived, query_weight.T, key_weight.T, value_weight.T, aug, hot,
        grad_context.T, g, cot.T, HEADS, share,
    )
    part = keep + exchange(send, "img", 0)
    half = part.shape[-1] // 2
    dims = (2,) * (bits - 1) + (share, half)
    parts = [part[:, :, :half].reshape(dims), part[:, :, half:].reshape(dims)]
    left = [list(reversed(range(1, bits))) for _ in parts]
    cut = halve(parts, "img", left, (1, 2))
    context, *kept = lax.optimization_barrier((context, cut[0][2], cut[1][2]))
    cut = [(keep, power, scaled) for (keep, power, _), scaled in zip(cut, kept)]
    parts = join(cut, "img", (1, 2))
    attended = out_side(arrived, out_weight, context)
    parts = join(halve(parts, "img", left, (2, 1)), "img", (2, 1))
    parts = [jnp.concatenate(parts, axis=-1)]
    left = left[:1]
    for bit in range(3, bits):
        parts = join(halve(parts, "img", left, (bit,)), "img", (bit,))
    return (attended[None], parts[0] * (1.0 / devices_img))


def solution(mesh):
    spread = P(("groups", "img"), None, None)
    placed = (spread, P("groups"), P("groups", None), spread, spread) + (P(),) * 5
    return jax.shard_map(
        per_device,
        mesh=mesh,
        in_specs=placed,
        out_specs=(spread, P(("groups", "img"), None)),
        check_vma=False,
    )
```

```python
import functools
import math

import jax
import jax.numpy as jnp
from jax import lax
from jax.experimental import pallas as pl
from jax.experimental.pallas import tpu as pltpu
from jax.sharding import PartitionSpec as P

HEADS = 8
BLOCK = 64
CHUNK = 256
GROUP = 512
DEAD = -1e30
F32 = jnp.float32
F16 = jnp.float16
BF16 = jnp.bfloat16
VMEM = pl.BlockSpec(memory_space=pltpu.VMEM)
HBM = pl.BlockSpec(memory_space=pltpu.HBM)
SMEM = pl.BlockSpec(memory_space=pltpu.SMEM)


def dot_nn(a, b):
    return lax.dot_general(a, b, (((1,), (0,)), ((), ())), preferred_element_type=F32)


def dot_nt(a, b):
    return lax.dot_general(a, b, (((1,), (1,)), ((), ())), preferred_element_type=F32)


def norm_columns(tokens):
    values_f = tokens.astype(F32)
    width = values_f.shape[0]
    centred = values_f - jnp.sum(values_f, axis=0, keepdims=True) * (1.0 / width)
    spread_sq = jnp.sum(centred * centred, axis=0, keepdims=True) * (1.0 / width)
    return (centred * lax.rsqrt(spread_sq + 1e-06)).astype(BF16)


def pick_body(owner_ref, pairs_ref, shares_ref, out_ref):
    for p in range(shares_ref.shape[0]):
        for side in range(2):
            out_ref[p, side] = shares_ref[owner_ref[pairs_ref[2 * p + side]]]


def pick(owner_slot, pairs, shares):
    count = shares.shape[0]
    return pl.pallas_call(
        pick_body,
        out_shape=jax.ShapeDtypeStruct((count, 2) + shares.shape[1:], shares.dtype),
        in_specs=[SMEM, SMEM, VMEM],
        out_specs=VMEM,
        compiler_params=pltpu.CompilerParams(vmem_limit_bytes=16 * 2**20),
        name="pick_shares",
    )(owner_slot, pairs.reshape(-1), shares)


def pair_body(
    heads, core_ref, token_in, qw_in, kw_in, vw_in, aug_in, hot_in, gt_in, cot_in,
    ctx_ref, keep_qk_ref, send_qk_ref, keep_vo_ref, send_vo_ref,
    token_ref, qw_ref, kw_ref, vw_ref, aug_ref, hot_ref, gt_ref, cot_ref,
    qn_ref, kn_ref, qt_ref, kt_ref, vt_ref, k_ref, v_ref, gq_ref, val_ref,
    token_sems, in_sems, out_sems,
):
    count, _, share, length = token_ref.shape
    att = qw_ref.shape[0]
    hsize = att // heads
    scale = jnp.asarray(1.0 / math.sqrt(hsize), BF16)
    chunks = [pl.ds(c * CHUNK, CHUNK) for c in range(length // CHUNK)]
    tokens_here = [
        pltpu.make_async_copy(
            token_in.at[:, :, :, cols], token_ref.at[:, :, :, cols], token_sems.at[c]
        )
        for c, cols in enumerate(chunks)
    ]
    in_pairs = (
        (qw_in, qw_ref), (kw_in, kw_ref), (vw_in, vw_ref), (aug_in, aug_ref), (hot_in, hot_ref),
        (gt_in, gt_ref), (cot_in, cot_ref),
    )
    others = [
        pltpu.make_async_copy(source, target, in_sems.at[n])
        for n, (source, target) in enumerate(in_pairs)
    ]
    for copy in tokens_here[:1] + others[:3] + tokens_here[1:] + others[3:]:
        copy.start()
    for c, cols in enumerate(chunks):
        tokens_here[c].wait()
        query_n = norm_columns(token_ref[:, 0, :, cols].reshape(count * share, CHUNK))
        key_n = norm_columns(token_ref[:, 1, :, cols].reshape(count * share, CHUNK))
        qn_ref[:, cols] = query_n
        kn_ref[:, cols] = key_n
        if c == 0:
            for copy in others[:3]:
                copy.wait()
        qt_ref[:, cols] = dot_nn(qw_ref[...], query_n).astype(BF16)
        kt_ref[:, cols] = dot_nn(kw_ref[...], key_n).astype(BF16)
        vt_ref[:, cols] = dot_nn(vw_ref[...], key_n).astype(BF16)
    for copy in others[3:]:
        copy.wait()
    for h in range(heads):
        rows = pl.ds(h * hsize, hsize)
        k_ref[h] = jnp.concatenate([kt_ref[rows, :].T, aug_ref[...]], axis=1)
        v_ref[h] = vt_ref[rows, :].T

    def rows_of(h):
        return pl.ds(h * hsize, hsize)

    def scores_of(h):
        query_aug = jnp.concatenate([qt_ref[rows_of(h), :] * scale, hot_ref[...]], axis=0)
        return dot_nn(k_ref[h], query_aug)

    def softmax(scores):
        weights = jnp.exp(scores - jnp.max(scores, axis=0, keepdims=True))
        return weights * (1.0 / jnp.sum(weights, axis=0, keepdims=True))

    def context_of(h, low):
        ctx_ref[rows_of(h), :] = dot_nn(vt_ref[rows_of(h), :], low).astype(BF16)
        return dot_nt(low, gt_ref[rows_of(h), :]).astype(BF16)

    def grad_score_of(prob, grad_prob):
        inner = jnp.sum(prob * grad_prob, axis=0, keepdims=True)
        return (prob * (grad_prob - inner)).astype(BF16)

    def grads_of(h, grad_score):
        gq_ref[rows_of(h), :] = dot_nn(kt_ref[rows_of(h), :], grad_score).astype(BF16)
        return dot_nt(grad_score, qt_ref[rows_of(h), :]).astype(BF16)

    def two_heads(i):
        pair = (2 * i, 2 * i + 1)
        scores = [scores_of(h) for h in pair]
        grad_probs = [dot_nn(v_ref[h], gt_ref[rows_of(h), :] * scale) for h in pair]
        probs = [softmax(each) for each in scores]
        grad_values = [context_of(h, prob.astype(BF16)) for h, prob in zip(pair, probs)]
        grad_scores = [grad_score_of(*each) for each in zip(probs, grad_probs)]
        return [grads_of(h, each) for h, each in zip(pair, grad_scores)], grad_values

    mine = core_ref[0]
    blocks, rows_each, _ = keep_qk_ref.shape
    group = val_ref.shape[-1]
    per_group = group // hsize
    outs = ((keep_qk_ref, send_qk_ref), (keep_vo_ref, send_vo_ref))

    def leaving(i, n, m):
        cols = pl.ds((n % 2) * att + i * group, group)
        return pltpu.make_async_copy(
            val_ref.at[i, n, :, mine if m == 0 else 1 - mine],
            outs[n // 2][m].at[:, :, cols],
            out_sems.at[i, n, m],
        )

    def one_group(i, carry):
        grad_keys, grad_values = [], []
        for j in range(per_group // 2):
            more_keys, more_values = two_heads(i * (per_group // 2) + j)
            grad_keys += more_keys
            grad_values += more_values
        rows = pl.ds(i * group, group)
        for n, grad in (
            (2, lambda: dot_nn(kn_ref[...], jnp.concatenate(grad_values, axis=1))),
            (3, lambda: dot_nt(cot_ref[...], ctx_ref[rows, :])),
            (1, lambda: dot_nn(kn_ref[...], jnp.concatenate(grad_keys, axis=1))),
            (0, lambda: dot_nt(qn_ref[...], gq_ref[rows, :])),
        ):
            grad = grad()
            if rows_each % 8:
                for b in range(2 * blocks):
                    block = grad[b * rows_each : (b + 1) * rows_each, :]
                    val_ref[i, n, b // 2, b % 2] = block
            else:
                val_ref[i, n] = grad.reshape(blocks, 2, rows_each, group)
            for m in range(2):
                leaving(i, n, m).start()
        return carry

    groups = att // group
    for i in range(groups):
        one_group(i, 0)
    for i in range(groups):
        for n in range(4):
            for m in range(2):
                leaving(i, n, m).wait()


def pair_side(core, arrived, qw, kw, vw, aug, hot, gt, cot, heads, rows_each):
    length = arrived.shape[-1]
    width = cot.shape[0]
    att = qw.shape[0]
    hsize = att // heads
    blocks = width // rows_each // 2
    part = jax.ShapeDtypeStruct((blocks, rows_each, 2 * att), F32)
    flat = pltpu.VMEM((att, length), BF16)
    square = pltpu.VMEM((width, length), BF16)
    inputs = (arrived, qw, kw, vw, aug, hot, gt, cot)
    return pl.pallas_call(
        functools.partial(pair_body, heads),
        out_shape=(jax.ShapeDtypeStruct((att, length), BF16), part, part, part, part),
        in_specs=[SMEM] + [HBM] * len(inputs),
        out_specs=(VMEM,) + (HBM,) * 4,
        scratch_shapes=[pltpu.VMEM(array.shape, array.dtype) for array in inputs]
        + [
            square,
            square,
            flat,
            flat,
            flat,
            pltpu.VMEM((heads, length, 2 * hsize), BF16),
            pltpu.VMEM((heads, length, hsize), BF16),
            flat,
            pltpu.VMEM((att // GROUP, 4, blocks, 2, rows_each, GROUP), F32),
            pltpu.SemaphoreType.DMA((length // CHUNK,)),
            pltpu.SemaphoreType.DMA((len(inputs) - 1,)),
            pltpu.SemaphoreType.DMA((att // GROUP, 4, 2)),
        ],
        compiler_params=pltpu.CompilerParams(vmem_limit_bytes=56 * 2**20),
        name="pair_pass",
    )(core, *inputs)


def exchange(array, axis, bit):
    size = lax.axis_size(axis)
    return lax.ppermute(array, axis, [(d, d ^ (1 << bit)) for d in range(size)])


def out_body(token_ref, ow_ref, ctx_ref, out_ref):
    count, _, share, length = token_ref.shape
    for c in range(length // CHUNK):
        cols = pl.ds(c * CHUNK, CHUNK)
        tokens = token_ref[:, 0, :, cols].reshape(count * share, CHUNK)
        summed = tokens.astype(F32) + dot_nn(ow_ref[...], ctx_ref[:, cols])
        out_ref[cols, :] = summed.astype(BF16).T


def out_side(arrived, ow, context):
    width, att = ow.shape
    length = context.shape[1]
    return pl.pallas_call(
        out_body,
        out_shape=jax.ShapeDtypeStruct((length, width), BF16),
        in_specs=[VMEM] * 3,
        out_specs=VMEM,
        compiler_params=pltpu.CompilerParams(vmem_limit_bytes=24 * 2**20),
        cost_estimate=pl.CostEstimate(
            flops=2 * width * att * length, bytes_accessed=6 * width * length, transcendentals=0
        ),
        name="attended_out",
    )(arrived, ow, context)


def halve(parts, axis, left, bits):
    me = lax.axis_index(axis)
    cut = []
    for part, lefts, bit in zip(parts, left, bits):
        at = lefts.index(bit)
        lefts.pop(at)
        mine = (me >> bit) & 1
        send = lax.dynamic_index_in_dim(part, 1 - mine, at, keepdims=False)
        keep = lax.dynamic_index_in_dim(part, mine, at, keepdims=False)
        top = jnp.max(jnp.abs(send), axis=tuple(range(send.ndim - 1)), keepdims=True)
        power = jnp.ceil(jnp.log2(jnp.maximum(top, 1e-30)))
        cut.append((keep, power, (send * jnp.exp2(8.0 - power)).astype(F16)))
    return cut


def join(cut, axis, bits):
    out = []
    for (keep, power, scaled), bit in zip(cut, bits):
        power = exchange(power, axis, bit)
        out.append(keep + exchange(scaled, axis, bit).astype(F32) * jnp.exp2(power - 8.0))
    return out


def per_device(
    caches, owner_slot, pairs, block_mask, cotangent, embed_weight, query_weight,
    key_weight, value_weight, out_weight,
):
    devices_img = lax.axis_size("img")
    bits = devices_img.bit_length() - 1
    length = caches.shape[1]
    width = embed_weight.shape[1]
    att = query_weight.shape[1]
    hsize = att // HEADS
    blocks = block_mask.shape[1]
    cot = cotangent[0]
    share = width // devices_img

    embedded = lax.dot_general(
        embed_weight, caches[0], (((0,), (1,)), ((), ())), preferred_element_type=F32
    ).astype(BF16)
    shares = lax.all_to_all(
        embedded.reshape(devices_img, share, length), "img", 0, 0, tiled=True
    )
    picked = pick(owner_slot, pairs, shares)
    arrived = lax.all_to_all(picked, "img", 0, 0, tiled=True)
    if share % 16:
        arrived = arrived.transpose(1, 0, 2, 3).reshape(1, 2, width, length)

    bias = jnp.where(block_mask[0] > 0, 0.0, DEAD).astype(BF16)
    aug = jnp.pad(jnp.repeat(bias.T, BLOCK, axis=0), ((0, 0), (0, hsize - blocks)))
    hot = (
        lax.broadcasted_iota(jnp.int32, (hsize, length), 0)
        == lax.broadcasted_iota(jnp.int32, (hsize, length), 1) // BLOCK
    ).astype(BF16)
    grad_context = jnp.dot(cot, out_weight, preferred_element_type=F32).astype(BF16)
    core = (lax.axis_index("img") % 2).astype(jnp.int32).reshape(1)

    context, keep_qk, send_qk, keep_vo, send_vo = pair_side(
        core, arrived, query_weight.T, key_weight.T, value_weight.T, aug, hot,
        grad_context.T, cot.T, HEADS, share,
    )
    parts = [keep_qk + exchange(send_qk, "img", 0), keep_vo + exchange(send_vo, "img", 0)]
    dims = (2,) * (bits - 1) + parts[0].shape[1:]
    parts = [part.reshape(dims) for part in parts]
    left = [list(reversed(range(1, bits))) for _ in parts]
    cut = halve(parts, "img", left, (1, 2))
    context = lax.optimization_barrier((context, cut[0][2], cut[1][2]))[0]
    parts = join(cut, "img", (1, 2))
    attended = out_side(arrived, out_weight, context)
    parts = join(halve(parts, "img", left, (2, 1)), "img", (2, 1))
    parts = [jnp.concatenate(parts, axis=-1)]
    left = left[:1]
    for bit in range(3, bits):
        parts = join(halve(parts, "img", left, (bit,)), "img", (bit,))
    return (attended[None], parts[0] * (1.0 / devices_img))


def solution(mesh):
    spread = P(("groups", "img"), None, None)
    placed = (spread, P("groups"), P("groups", None), spread, spread) + (P(),) * 5
    return jax.shard_map(
        per_device,
        mesh=mesh,
        in_specs=placed,
        out_specs=(spread, P(("groups", "img"), None)),
        check_vma=False,
    )
```

```python
import functools
import math

import jax
import jax.numpy as jnp
from jax import lax
from jax.experimental import pallas as pl
from jax.experimental.pallas import tpu as pltpu
from jax.sharding import PartitionSpec as P

HEADS = 8
BLOCK = 64
CHUNK = 256
GROUP = 512
POWER_ROWS = 8
DEAD = -1e30
F32 = jnp.float32
F16 = jnp.float16
BF16 = jnp.bfloat16
VMEM = pl.BlockSpec(memory_space=pltpu.VMEM)
HBM = pl.BlockSpec(memory_space=pltpu.HBM)
SMEM = pl.BlockSpec(memory_space=pltpu.SMEM)


def dot_nn(a, b):
    return lax.dot_general(a, b, (((1,), (0,)), ((), ())), preferred_element_type=F32)


def dot_nt(a, b):
    return lax.dot_general(a, b, (((1,), (1,)), ((), ())), preferred_element_type=F32)


def norm_columns(tokens):
    values_f = tokens.astype(F32)
    width = values_f.shape[0]
    centred = values_f - jnp.sum(values_f, axis=0, keepdims=True) * (1.0 / width)
    spread_sq = jnp.sum(centred * centred, axis=0, keepdims=True) * (1.0 / width)
    return (centred * lax.rsqrt(spread_sq + 1e-06)).astype(BF16)


def pick_body(owner_ref, pairs_ref, shares_ref, out_ref):
    for p in range(shares_ref.shape[0]):
        for side in range(2):
            out_ref[p, side] = shares_ref[owner_ref[pairs_ref[2 * p + side]]]


def pick(owner_slot, pairs, shares):
    count = shares.shape[0]
    return pl.pallas_call(
        pick_body,
        out_shape=jax.ShapeDtypeStruct((count, 2) + shares.shape[1:], shares.dtype),
        in_specs=[SMEM, SMEM, VMEM],
        out_specs=VMEM,
        compiler_params=pltpu.CompilerParams(vmem_limit_bytes=16 * 2**20),
        name="pick_shares",
    )(owner_slot, pairs.reshape(-1), shares)


def pair_body(
    heads, core_ref, token_in, qw_in, kw_in, vw_in, aug_in, hot_in, gt_in, cot_in,
    ctx_ref, keep_qk_ref, send_qk_ref, keep_vo_ref, send_vo_ref,
    token_ref, qw_ref, kw_ref, vw_ref, aug_ref, hot_ref, gt_ref, cot_ref,
    qn_ref, kn_ref, qt_ref, kt_ref, vt_ref, k_ref, v_ref, gq_ref, val_ref,
    token_sems, in_sems, out_sems,
):
    count, _, share, length = token_ref.shape
    att = qw_ref.shape[0]
    hsize = att // heads
    scale = jnp.asarray(1.0 / math.sqrt(hsize), BF16)
    chunks = [pl.ds(c * CHUNK, CHUNK) for c in range(length // CHUNK)]
    tokens_here = [
        pltpu.make_async_copy(
            token_in.at[:, :, :, cols], token_ref.at[:, :, :, cols], token_sems.at[c]
        )
        for c, cols in enumerate(chunks)
    ]
    in_pairs = (
        (qw_in, qw_ref), (kw_in, kw_ref), (vw_in, vw_ref), (aug_in, aug_ref), (hot_in, hot_ref),
        (gt_in, gt_ref), (cot_in, cot_ref),
    )
    others = [
        pltpu.make_async_copy(source, target, in_sems.at[n])
        for n, (source, target) in enumerate(in_pairs)
    ]
    for copy in tokens_here[:1] + others[:3] + tokens_here[1:] + others[3:]:
        copy.start()
    for c, cols in enumerate(chunks):
        tokens_here[c].wait()
        query_n = norm_columns(token_ref[:, 0, :, cols].reshape(count * share, CHUNK))
        key_n = norm_columns(token_ref[:, 1, :, cols].reshape(count * share, CHUNK))
        qn_ref[:, cols] = query_n
        kn_ref[:, cols] = key_n
        if c == 0:
            for copy in others[:3]:
                copy.wait()
        qt_ref[:, cols] = dot_nn(qw_ref[...], query_n).astype(BF16)
        kt_ref[:, cols] = dot_nn(kw_ref[...], key_n).astype(BF16)
        vt_ref[:, cols] = dot_nn(vw_ref[...], key_n).astype(BF16)
    for copy in others[3:]:
        copy.wait()
    for h in range(heads):
        rows = pl.ds(h * hsize, hsize)
        k_ref[h] = jnp.concatenate([kt_ref[rows, :].T, aug_ref[...]], axis=1)
        v_ref[h] = vt_ref[rows, :].T

    def rows_of(h):
        return pl.ds(h * hsize, hsize)

    def scores_of(h):
        query_aug = jnp.concatenate([qt_ref[rows_of(h), :] * scale, hot_ref[...]], axis=0)
        return dot_nn(k_ref[h], query_aug)

    def softmax(scores):
        weights = jnp.exp(scores - jnp.max(scores, axis=0, keepdims=True))
        return weights * (1.0 / jnp.sum(weights, axis=0, keepdims=True))

    def context_of(h, low):
        ctx_ref[rows_of(h), :] = dot_nn(vt_ref[rows_of(h), :], low).astype(BF16)
        return dot_nt(low, gt_ref[rows_of(h), :]).astype(BF16)

    def grad_score_of(prob, grad_prob):
        inner = jnp.sum(prob * grad_prob, axis=0, keepdims=True)
        return (prob * (grad_prob - inner)).astype(BF16)

    def grads_of(h, grad_score):
        gq_ref[rows_of(h), :] = dot_nn(kt_ref[rows_of(h), :], grad_score).astype(BF16)
        return dot_nt(grad_score, qt_ref[rows_of(h), :]).astype(BF16)

    mine = core_ref[0]
    blocks, rows_each, _ = keep_qk_ref.shape
    group = val_ref.shape[-1]
    per_group = group // hsize
    outs = ((keep_qk_ref, send_qk_ref), (keep_vo_ref, send_vo_ref))

    def leaving(i, n, m):
        cols = pl.ds((n % 2) * att + i * group, group)
        return pltpu.make_async_copy(
            val_ref.at[i, n, :, mine if m == 0 else 1 - mine],
            outs[n // 2][m].at[:, :, cols],
            out_sems.at[i, n, m],
        )

    def send_out(n, grad):
        if rows_each % 8:
            for b in range(2 * blocks):
                block = grad[b * rows_each : (b + 1) * rows_each, :]
                val_ref[0, n, b // 2, b % 2] = block
        else:
            val_ref[0, n] = grad.reshape(blocks, 2, rows_each, group)
        for m in range(2):
            leaving(0, n, m).start()

    def products(some):
        scores = [scores_of(h) for h in some]
        return scores, [dot_nn(v_ref[h], gt_ref[rows_of(h), :] * scale) for h in some]

    grad_keys, grad_values = [], []
    together = [tuple(range(h, h + 1)) for h in range(0, heads, 1)]
    ahead = products(together[0])
    for n, some in enumerate(together):
        scores, grad_probs = ahead
        probs = [softmax(each) for each in scores]
        if n + 1 < len(together):
            ahead = products(together[n + 1])
        grad_values += [context_of(h, prob.astype(BF16)) for h, prob in zip(some, probs)]
        if n + 1 == len(together):
            send_out(2, dot_nn(kn_ref[...], jnp.concatenate(grad_values, axis=1)))
            send_out(3, dot_nt(cot_ref[...], ctx_ref[...]))
        grad_scores = [grad_score_of(*each) for each in zip(probs, grad_probs)]
        grad_keys += [grads_of(h, each) for h, each in zip(some, grad_scores)]
    send_out(1, dot_nn(kn_ref[...], jnp.concatenate(grad_keys, axis=1)))
    send_out(0, dot_nt(qn_ref[...], gq_ref[...]))
    groups = 1
    for i in range(groups):
        for n in range(4):
            for m in range(2):
                leaving(i, n, m).wait()


def pair_side(core, arrived, qw, kw, vw, aug, hot, gt, cot, heads, rows_each):
    length = arrived.shape[-1]
    width = cot.shape[0]
    att = qw.shape[0]
    hsize = att // heads
    blocks = width // rows_each // 2
    part = jax.ShapeDtypeStruct((blocks, rows_each, 2 * att), F32)
    flat = pltpu.VMEM((att, length), BF16)
    square = pltpu.VMEM((width, length), BF16)
    inputs = (arrived, qw, kw, vw, aug, hot, gt, cot)
    return pl.pallas_call(
        functools.partial(pair_body, heads),
        out_shape=(jax.ShapeDtypeStruct((att, length), BF16), part, part, part, part),
        in_specs=[SMEM] + [HBM] * len(inputs),
        out_specs=(VMEM,) + (HBM,) * 4,
        scratch_shapes=[pltpu.VMEM(array.shape, array.dtype) for array in inputs]
        + [
            square,
            square,
            flat,
            flat,
            flat,
            pltpu.VMEM((heads, length, 2 * hsize), BF16),
            pltpu.VMEM((heads, length, hsize), BF16),
            flat,
            pltpu.VMEM((att // GROUP, 4, blocks, 2, rows_each, GROUP), F32),
            pltpu.SemaphoreType.DMA((length // CHUNK,)),
            pltpu.SemaphoreType.DMA((len(inputs) - 1,)),
            pltpu.SemaphoreType.DMA((att // GROUP, 4, 2)),
        ],
        compiler_params=pltpu.CompilerParams(vmem_limit_bytes=56 * 2**20),
        name="pair_pass",
    )(core, *inputs)


def exchange(array, axis, bit):
    size = lax.axis_size(axis)
    return lax.ppermute(array, axis, [(d, d ^ (1 << bit)) for d in range(size)])


def out_body(token_ref, ow_ref, ctx_ref, out_ref):
    count, _, share, length = token_ref.shape
    for c in range(length // CHUNK):
        cols = pl.ds(c * CHUNK, CHUNK)
        tokens = token_ref[:, 0, :, cols].reshape(count * share, CHUNK)
        summed = tokens.astype(F32) + dot_nn(ow_ref[...], ctx_ref[:, cols])
        out_ref[cols, :] = summed.astype(BF16).T


def out_side(arrived, ow, context):
    width, att = ow.shape
    length = context.shape[1]
    return pl.pallas_call(
        out_body,
        out_shape=jax.ShapeDtypeStruct((length, width), BF16),
        in_specs=[VMEM] * 3,
        out_specs=VMEM,
        compiler_params=pltpu.CompilerParams(vmem_limit_bytes=24 * 2**20),
        cost_estimate=pl.CostEstimate(
            flops=2 * width * att * length, bytes_accessed=6 * width * length, transcendentals=0
        ),
        name="attended_out",
    )(arrived, ow, context)


def halve(parts, axis, left, bits):
    me = lax.axis_index(axis)
    cut = []
    for part, lefts, bit in zip(parts, left, bits):
        at = lefts.index(bit)
        lefts.pop(at)
        mine = (me >> bit) & 1
        send = lax.dynamic_index_in_dim(part, 1 - mine, at, keepdims=False)
        keep = lax.dynamic_index_in_dim(part, mine, at, keepdims=False)
        top = jnp.max(jnp.abs(send), axis=tuple(range(send.ndim - 1)), keepdims=True)
        power = jnp.ceil(jnp.log2(jnp.maximum(top, 1e-30)))
        cols = send.shape[-1]
        scaled = (send * jnp.exp2(8.0 - power)).astype(F16).reshape(-1, cols)
        powers = jnp.broadcast_to(power.astype(F16).reshape(1, cols), (POWER_ROWS, cols))
        cut.append((keep, jnp.concatenate([scaled, powers], axis=0)))
    return cut


def join(cut, axis, bits):
    out = []
    for (keep, message), bit in zip(cut, bits):
        got = exchange(message, axis, bit).astype(F32)
        factor = jnp.exp2(got[-1:] - 8.0)
        out.append(keep + (got[:-POWER_ROWS] * factor).reshape(keep.shape))
    return out


def per_device(
    caches, owner_slot, pairs, block_mask, cotangent, embed_weight, query_weight,
    key_weight, value_weight, out_weight,
):
    devices_img = lax.axis_size("img")
    bits = devices_img.bit_length() - 1
    length = caches.shape[1]
    width = embed_weight.shape[1]
    att = query_weight.shape[1]
    hsize = att // HEADS
    blocks = block_mask.shape[1]
    cot = cotangent[0]
    share = width // devices_img

    embedded = lax.dot_general(
        embed_weight, caches[0], (((0,), (1,)), ((), ())), preferred_element_type=F32
    ).astype(BF16)
    shares = lax.all_to_all(
        embedded.reshape(devices_img, share, length), "img", 0, 0, tiled=True
    )
    picked = pick(owner_slot, pairs, shares)
    arrived = lax.all_to_all(picked, "img", 0, 0, tiled=True)
    if share % 16:
        arrived = arrived.transpose(1, 0, 2, 3).reshape(1, 2, width, length)

    bias = jnp.where(block_mask[0] > 0, 0.0, DEAD).astype(BF16)
    aug = jnp.pad(jnp.repeat(bias.T, BLOCK, axis=0), ((0, 0), (0, hsize - blocks)))
    hot = (
        lax.broadcasted_iota(jnp.int32, (hsize, length), 0)
        == lax.broadcasted_iota(jnp.int32, (hsize, length), 1) // BLOCK
    ).astype(BF16)
    grad_context = jnp.dot(cot, out_weight, preferred_element_type=F32).astype(BF16)
    core = (lax.axis_index("img") % 2).astype(jnp.int32).reshape(1)

    context, keep_qk, send_qk, keep_vo, send_vo = pair_side(
        core, arrived, query_weight.T, key_weight.T, value_weight.T, aug, hot,
        grad_context.T, cot.T, HEADS, share,
    )
    batches = []
    for keep, send in ((keep_vo, send_vo), (keep_qk, send_qk)):
        part = keep + exchange(send, "img", 0)
        half = part.shape[-1] // 2
        dims = (2,) * (bits - 1) + (share, half)
        batches.append([part[:, :, :half].reshape(dims), part[:, :, half:].reshape(dims)])
    lefts = [[list(reversed(range(1, bits))) for _ in range(2)] for _ in batches]
    cuts = [halve(parts, "img", left, (1, 2)) for parts, left in zip(batches, lefts)]
    context = lax.optimization_barrier((context, cuts[1][0][1], cuts[1][1][1]))[0]
    attended = out_side(arrived, out_weight, context)
    sums = []
    for cut, left in zip(cuts, lefts):
        parts = join(cut, "img", (1, 2))
        parts = join(halve(parts, "img", left, (2, 1)), "img", (2, 1))
        parts = [jnp.concatenate(parts, axis=-1)]
        for bit in range(3, bits):
            parts = join(halve(parts, "img", left[:1], (bit,)), "img", (bit,))
        sums.append(parts[0])
    summed = jnp.concatenate([sums[1], sums[0]], axis=-1)
    return (attended[None], summed * (1.0 / devices_img))


def solution(mesh):
    spread = P(("groups", "img"), None, None)
    placed = (spread, P("groups"), P("groups", None), spread, spread) + (P(),) * 5
    return jax.shard_map(
        per_device,
        mesh=mesh,
        in_specs=placed,
        out_specs=(spread, P(("groups", "img"), None)),
        check_vma=False,
    )
```

```python
import functools
import math

import jax
import jax.numpy as jnp
from jax import lax
from jax.experimental import pallas as pl
from jax.experimental.pallas import tpu as pltpu
from jax.sharding import PartitionSpec as P

HEADS = 8
BLOCK = 64
CHUNK = 256
GROUP = 512
POWER_ROWS = 8
DEAD = -1e30
F32 = jnp.float32
F16 = jnp.float16
BF16 = jnp.bfloat16
VMEM = pl.BlockSpec(memory_space=pltpu.VMEM)
HBM = pl.BlockSpec(memory_space=pltpu.HBM)
SMEM = pl.BlockSpec(memory_space=pltpu.SMEM)


def dot_nn(a, b):
    return lax.dot_general(a, b, (((1,), (0,)), ((), ())), preferred_element_type=F32)


def dot_nt(a, b):
    return lax.dot_general(a, b, (((1,), (1,)), ((), ())), preferred_element_type=F32)


def norm_columns(tokens):
    values_f = tokens.astype(F32)
    width = values_f.shape[0]
    centred = values_f - jnp.sum(values_f, axis=0, keepdims=True) * (1.0 / width)
    spread_sq = jnp.sum(centred * centred, axis=0, keepdims=True) * (1.0 / width)
    return (centred * lax.rsqrt(spread_sq + 1e-06)).astype(BF16)


def pick_body(owner_ref, pairs_ref, shares_ref, out_ref):
    for p in range(shares_ref.shape[0]):
        for side in range(2):
            out_ref[p, side] = shares_ref[owner_ref[pairs_ref[2 * p + side]]]


def pick(owner_slot, pairs, shares):
    count = shares.shape[0]
    return pl.pallas_call(
        pick_body,
        out_shape=jax.ShapeDtypeStruct((count, 2) + shares.shape[1:], shares.dtype),
        in_specs=[SMEM, SMEM, VMEM],
        out_specs=VMEM,
        compiler_params=pltpu.CompilerParams(vmem_limit_bytes=16 * 2**20),
        name="pick_shares",
    )(owner_slot, pairs.reshape(-1), shares)


def pair_body(
    heads, core_ref, token_in, qw_in, kw_in, vw_in, aug_in, hot_in, gt_in, cot_in,
    ctx_ref, keep_qk_ref, send_qk_ref, keep_vo_ref, send_vo_ref,
    token_ref, qw_ref, kw_ref, vw_ref, aug_ref, hot_ref, gt_ref, cot_ref,
    qn_ref, kn_ref, qt_ref, kt_ref, vt_ref, k_ref, v_ref, gq_ref, val_ref,
    token_sems, in_sems, out_sems,
):
    count, _, share, length = token_ref.shape
    att = qw_ref.shape[0]
    hsize = att // heads
    scale = jnp.asarray(1.0 / math.sqrt(hsize), BF16)
    chunks = [pl.ds(c * CHUNK, CHUNK) for c in range(length // CHUNK)]
    tokens_here = [
        pltpu.make_async_copy(
            token_in.at[:, :, :, cols], token_ref.at[:, :, :, cols], token_sems.at[c]
        )
        for c, cols in enumerate(chunks)
    ]
    in_pairs = (
        (qw_in, qw_ref), (kw_in, kw_ref), (vw_in, vw_ref), (aug_in, aug_ref), (hot_in, hot_ref),
        (gt_in, gt_ref), (cot_in, cot_ref),
    )
    others = [
        pltpu.make_async_copy(source, target, in_sems.at[n])
        for n, (source, target) in enumerate(in_pairs)
    ]
    for copy in tokens_here[:1] + others[:3] + tokens_here[1:] + others[3:]:
        copy.start()
    for c, cols in enumerate(chunks):
        tokens_here[c].wait()
        query_n = norm_columns(token_ref[:, 0, :, cols].reshape(count * share, CHUNK))
        key_n = norm_columns(token_ref[:, 1, :, cols].reshape(count * share, CHUNK))
        qn_ref[:, cols] = query_n
        kn_ref[:, cols] = key_n
        if c == 0:
            for copy in others[:3]:
                copy.wait()
        qt_ref[:, cols] = dot_nn(qw_ref[...], query_n).astype(BF16)
        kt_ref[:, cols] = dot_nn(kw_ref[...], key_n).astype(BF16)
        vt_ref[:, cols] = dot_nn(vw_ref[...], key_n).astype(BF16)
    for copy in others[3:]:
        copy.wait()
    for h in range(heads):
        rows = pl.ds(h * hsize, hsize)
        k_ref[h] = jnp.concatenate([kt_ref[rows, :].T, aug_ref[...]], axis=1)
        v_ref[h] = vt_ref[rows, :].T

    def rows_of(h):
        return pl.ds(h * hsize, hsize)

    def scores_of(h):
        query_aug = jnp.concatenate([qt_ref[rows_of(h), :] * scale, hot_ref[...]], axis=0)
        return dot_nn(k_ref[h], query_aug)

    def softmax(scores):
        weights = jnp.exp(scores - jnp.max(scores, axis=0, keepdims=True))
        return weights * (1.0 / jnp.sum(weights, axis=0, keepdims=True))

    def context_of(h, low):
        ctx_ref[rows_of(h), :] = dot_nn(vt_ref[rows_of(h), :], low).astype(BF16)
        return dot_nt(low, gt_ref[rows_of(h), :]).astype(BF16)

    def grad_score_of(prob, grad_prob):
        inner = jnp.sum(prob * grad_prob, axis=0, keepdims=True)
        return (prob * (grad_prob - inner)).astype(BF16)

    def grads_of(h, grad_score):
        gq_ref[rows_of(h), :] = dot_nn(kt_ref[rows_of(h), :], grad_score).astype(BF16)
        return dot_nt(grad_score, qt_ref[rows_of(h), :]).astype(BF16)

    mine = core_ref[0]
    blocks, rows_each, _ = keep_qk_ref.shape
    group = val_ref.shape[-1]
    per_group = group // hsize
    outs = ((keep_qk_ref, send_qk_ref), (keep_vo_ref, send_vo_ref))

    def leaving(i, n, m):
        cols = pl.ds((n % 2) * att + i * group, group)
        return pltpu.make_async_copy(
            val_ref.at[i, n, :, mine if m == 0 else 1 - mine],
            outs[n // 2][m].at[:, :, cols],
            out_sems.at[i, n, m],
        )

    def send_out(n, grad):
        if rows_each % 8:
            for b in range(2 * blocks):
                block = grad[b * rows_each : (b + 1) * rows_each, :]
                val_ref[0, n, b // 2, b % 2] = block
        else:
            val_ref[0, n] = grad.reshape(blocks, 2, rows_each, group)
        for m in range(2):
            leaving(0, n, m).start()

    def products(some):
        scores = [scores_of(h) for h in some]
        return scores, [dot_nn(v_ref[h], gt_ref[rows_of(h), :] * scale) for h in some]

    grad_keys, grad_values = [], []
    together = [tuple(range(h, h + 1)) for h in range(0, heads, 1)]
    ahead = products(together[0])
    for n, some in enumerate(together):
        scores, grad_probs = ahead
        probs = [softmax(each) for each in scores]
        if n + 1 < len(together):
            ahead = products(together[n + 1])
        grad_values += [context_of(h, prob.astype(BF16)) for h, prob in zip(some, probs)]
        if n + 1 == len(together):
            send_out(2, dot_nn(kn_ref[...], jnp.concatenate(grad_values, axis=1)))
            send_out(3, dot_nt(cot_ref[...], ctx_ref[...]))
        grad_scores = [grad_score_of(*each) for each in zip(probs, grad_probs)]
        grad_keys += [grads_of(h, each) for h, each in zip(some, grad_scores)]
    send_out(1, dot_nn(kn_ref[...], jnp.concatenate(grad_keys, axis=1)))
    send_out(0, dot_nt(qn_ref[...], gq_ref[...]))
    groups = 1
    for i in range(groups):
        for n in range(4):
            for m in range(2):
                leaving(i, n, m).wait()


def pair_side(core, arrived, qw, kw, vw, aug, hot, gt, cot, heads, rows_each):
    length = arrived.shape[-1]
    width = cot.shape[0]
    att = qw.shape[0]
    hsize = att // heads
    blocks = width // rows_each // 2
    part = jax.ShapeDtypeStruct((blocks, rows_each, 2 * att), F32)
    flat = pltpu.VMEM((att, length), BF16)
    square = pltpu.VMEM((width, length), BF16)
    inputs = (arrived, qw, kw, vw, aug, hot, gt, cot)
    return pl.pallas_call(
        functools.partial(pair_body, heads),
        out_shape=(jax.ShapeDtypeStruct((att, length), BF16), part, part, part, part),
        in_specs=[SMEM] + [HBM] * len(inputs),
        out_specs=(VMEM,) + (HBM,) * 4,
        scratch_shapes=[pltpu.VMEM(array.shape, array.dtype) for array in inputs]
        + [
            square,
            square,
            flat,
            flat,
            flat,
            pltpu.VMEM((heads, length, 2 * hsize), BF16),
            pltpu.VMEM((heads, length, hsize), BF16),
            flat,
            pltpu.VMEM((att // GROUP, 4, blocks, 2, rows_each, GROUP), F32),
            pltpu.SemaphoreType.DMA((length // CHUNK,)),
            pltpu.SemaphoreType.DMA((len(inputs) - 1,)),
            pltpu.SemaphoreType.DMA((att // GROUP, 4, 2)),
        ],
        compiler_params=pltpu.CompilerParams(vmem_limit_bytes=56 * 2**20),
        name="pair_pass",
    )(core, *inputs)


def exchange(array, axis, bit):
    size = lax.axis_size(axis)
    return lax.ppermute(array, axis, [(d, d ^ (1 << bit)) for d in range(size)])


def out_body(token_ref, ow_ref, ctx_ref, out_ref):
    count, _, share, length = token_ref.shape
    for c in range(length // CHUNK):
        cols = pl.ds(c * CHUNK, CHUNK)
        tokens = token_ref[:, 0, :, cols].reshape(count * share, CHUNK)
        summed = tokens.astype(F32) + dot_nn(ow_ref[...], ctx_ref[:, cols])
        out_ref[cols, :] = summed.astype(BF16).T


def out_side(arrived, ow, context):
    width, att = ow.shape
    length = context.shape[1]
    return pl.pallas_call(
        out_body,
        out_shape=jax.ShapeDtypeStruct((length, width), BF16),
        in_specs=[VMEM] * 3,
        out_specs=VMEM,
        compiler_params=pltpu.CompilerParams(vmem_limit_bytes=24 * 2**20),
        cost_estimate=pl.CostEstimate(
            flops=2 * width * att * length, bytes_accessed=6 * width * length, transcendentals=0
        ),
        name="attended_out",
    )(arrived, ow, context)


def halve(parts, axis, left, bits):
    me = lax.axis_index(axis)
    cut = []
    for part, lefts, bit in zip(parts, left, bits):
        at = lefts.index(bit)
        lefts.pop(at)
        mine = (me >> bit) & 1
        send = lax.dynamic_index_in_dim(part, 1 - mine, at, keepdims=False)
        keep = lax.dynamic_index_in_dim(part, mine, at, keepdims=False)
        top = jnp.max(jnp.abs(send), axis=tuple(range(send.ndim - 1)), keepdims=True)
        power = jnp.ceil(jnp.log2(jnp.maximum(top, 1e-30)))
        cols = send.shape[-1]
        scaled = (send * jnp.exp2(8.0 - power)).astype(F16).reshape(-1, cols)
        powers = jnp.broadcast_to(power.astype(F16).reshape(1, cols), (POWER_ROWS, cols))
        cut.append((keep, jnp.concatenate([scaled, powers], axis=0)))
    return cut


def join(cut, axis, bits):
    out = []
    for (keep, message), bit in zip(cut, bits):
        got = exchange(message, axis, bit).astype(F32)
        factor = jnp.exp2(got[-1:] - 8.0)
        out.append(keep + (got[:-POWER_ROWS] * factor).reshape(keep.shape))
    return out


def per_device(
    caches, owner_slot, pairs, block_mask, cotangent, embed_weight, query_weight,
    key_weight, value_weight, out_weight,
):
    devices_img = lax.axis_size("img")
    bits = devices_img.bit_length() - 1
    length = caches.shape[1]
    width = embed_weight.shape[1]
    att = query_weight.shape[1]
    hsize = att // HEADS
    blocks = block_mask.shape[1]
    cot = cotangent[0]
    share = width // devices_img

    embedded = lax.dot_general(
        embed_weight, caches[0], (((0,), (1,)), ((), ())), preferred_element_type=F32
    ).astype(BF16)
    shares = lax.all_to_all(
        embedded.reshape(devices_img, share, length), "img", 0, 0, tiled=True
    )
    picked = pick(owner_slot, pairs, shares)
    arrived = lax.all_to_all(picked, "img", 0, 0, tiled=True)
    if share % 16:
        arrived = arrived.transpose(1, 0, 2, 3).reshape(1, 2, width, length)

    bias = jnp.where(block_mask[0] > 0, 0.0, DEAD).astype(BF16)
    aug = jnp.pad(jnp.repeat(bias.T, BLOCK, axis=0), ((0, 0), (0, hsize - blocks)))
    hot = (
        lax.broadcasted_iota(jnp.int32, (hsize, length), 0)
        == lax.broadcasted_iota(jnp.int32, (hsize, length), 1) // BLOCK
    ).astype(BF16)
    grad_context = jnp.dot(cot, out_weight, preferred_element_type=F32).astype(BF16)
    core = (lax.axis_index("img") % 2).astype(jnp.int32).reshape(1)

    context, keep_qk, send_qk, keep_vo, send_vo = pair_side(
        core, arrived, query_weight.T, key_weight.T, value_weight.T, aug, hot,
        grad_context.T, cot.T, HEADS, share,
    )
    batches = []
    for keep, send in ((keep_vo, send_vo), (keep_qk, send_qk)):
        part = keep + exchange(send, "img", 0)
        half = part.shape[-1] // 2
        dims = (2,) * (bits - 1) + (share, half)
        batches.append([part[:, :, :half].reshape(dims), part[:, :, half:].reshape(dims)])
    lefts = [[list(reversed(range(1, bits))) for _ in range(2)] for _ in batches]
    cuts = [halve(parts, "img", left, (1, 2)) for parts, left in zip(batches, lefts)]
    sums = []
    for cut, left in zip(cuts, lefts):
        parts = join(cut, "img", (1, 2))
        second = halve(parts, "img", left, (2, 1))
        parts = join(second, "img", (2, 1))
        parts = [jnp.concatenate(parts, axis=-1)]
        for bit in range(3, bits):
            parts = join(halve(parts, "img", left[:1], (bit,)), "img", (bit,))
        sums.append(parts[0])
    context = lax.optimization_barrier((context, second[0][1], second[1][1]))[0]
    attended = out_side(arrived, out_weight, context)
    summed = jnp.concatenate([sums[1], sums[0]], axis=-1)
    return (attended[None], summed * (1.0 / devices_img))


def solution(mesh):
    spread = P(("groups", "img"), None, None)
    placed = (spread, P("groups"), P("groups", None), spread, spread) + (P(),) * 5
    return jax.shard_map(
        per_device,
        mesh=mesh,
        in_specs=placed,
        out_specs=(spread, P(("groups", "img"), None)),
        check_vma=False,
    )
```
